256 devices in a mesh: row: 32 (over y, z), col: 8 (over x, core).
Axes of the slice: x: 4, y: 4, z: 8, core: 2. Of those that a mesh axis runs over, the one named last changes fastest.
Arguments:
- window: float32 [8192, 8192], P('row', 'col'), may hold values from -6 to 6
- leaf_y: float32 [2, 8192, 256], P(None, 'row', 'col'), may hold values from -6 to 6
- tree_y: float32 [2, 5, 8192, 256], P(None, None, 'row', 'col'), may hold values from -6 to 6
Outputs:
- updated: float32 [8192, 8192], P('row', 'col')
The draws below stay inside these ranges and needn't reach their ends.
All inputs are finite; a program needn't handle non-finite values.
Results may differ from the reference program's by a relative error of at most 0.0003.
Values sent between devices are 32-bit elements; how exact they have to be, the bound alone decides.
A program may use at most 128 MiB of HBM per device.

```python
import jax
import jax.numpy as jnp
import numpy as np
from jax import lax

B = 256
NC = 8192
R = 256
M = 8192
LEVELS = 5
N_ROW = 32


def shard_levels(stream_key, dims, shards, low, largest):
    gain, own = 1.0, jax.random.fold_in(stream_key, 6)
    for axis_at, blocks in shards:
        steps = jnp.exp(jax.random.uniform(jax.random.fold_in(own, axis_at), (blocks,), jnp.float32, low / len(shards), largest / len(shards)))
        gain = gain * jnp.repeat(steps, dims[axis_at] // blocks).reshape([-1 if axis == axis_at else 1 for axis in range(len(dims))])
    return gain


def normal_values(stream_key, dims, deviation, limit, cuts=(), held_as=jnp.bfloat16):
    drawn = deviation * jax.random.normal(stream_key, dims, jnp.float32)
    if cuts:
        drawn = drawn * shard_levels(stream_key, dims, cuts, -0.22, 0.18)
    return jnp.clip(drawn, -limit, limit).astype(held_as)


def setup_inputs(seed: int = 0) -> dict:
    arg_keys = jax.random.split(jax.random.key(seed), 4)
    return {
        "window": normal_values(arg_keys[0], (M, NC), 1.0, 6.0, ((0, 32), (1, 8)), jnp.float32),
        "leaf_y": normal_values(arg_keys[1], (2, M, B), 1.0, 6.0, ((1, 32), (2, 8)), jnp.float32),
        "tree_y": normal_values(arg_keys[2], (2, LEVELS, N_ROW * B, B), 1.0, 6.0, ((2, 32), (3, 8)), jnp.float32),
    }


def triangle(gramian):
    return jnp.triu(gramian, 1) + jnp.diag(jnp.diag(gramian)) * 0.5

def reflect(matrix_block, vectors, gramian, inners):
    coefficients = jax.scipy.linalg.solve_triangular(triangle(gramian), inners, trans=1, lower=False)
    return matrix_block - jnp.dot(vectors.astype(jnp.float32), coefficients.astype(jnp.float32), precision=lax.Precision.HIGHEST, preferred_element_type=jnp.float32)

def leaf_step(paired):
    matrix_block, vectors = paired
    gramian = jnp.dot(vectors.T.astype(jnp.float32), vectors.astype(jnp.float32), precision=lax.Precision.HIGHEST, preferred_element_type=jnp.float32)
    inners = jnp.dot(vectors.T.astype(jnp.float32), matrix_block.astype(jnp.float32), precision=lax.Precision.HIGHEST, preferred_element_type=jnp.float32)
    return reflect(matrix_block, vectors, gramian, inners)

def reference(window, leaf_y, tree_y):
    blocks = window.reshape(N_ROW, R, NC)
    for panel_index in range(2):
        vectors = leaf_y[panel_index].reshape(N_ROW, R, B)
        blocks = lax.map(leaf_step, (blocks, vectors))
        for level_index in range(LEVELS):
            partner = np.arange(N_ROW) ^ 1 << level_index
            tree_vectors = tree_y[panel_index, level_index].reshape(N_ROW, B, B)
            top_rows = blocks[:, :B]
            gramians = jnp.einsum('nki,nkj->nij', tree_vectors, tree_vectors, precision=lax.Precision.HIGHEST)
            inners = jnp.einsum('nki,nkj->nij', tree_vectors, top_rows, precision=lax.Precision.HIGHEST)
            gram_total = gramians + gramians[partner]
            inner_total = inners + inners[partner]
            new_top = jax.vmap(reflect)(top_rows, tree_vectors, gram_total, inner_total)
            blocks = blocks.at[:, :B].set(new_top)
    return blocks.reshape(N_ROW * R, NC)
```

```python
import functools

import jax
import jax.numpy as jnp
from jax import lax
from jax.experimental import pallas as pl
from jax.experimental.pallas import tpu as pltpu
from jax.sharding import PartitionSpec as P

F32 = jnp.float32
BF16 = jnp.bfloat16
CHUNKS = 4
LEVELS = 5


def dims(ta, tb):
    return (((0,) if ta else (1,), (1,) if tb else (0,)), ((), ()))


def full_dot(a, b, ta=False, tb=False):
    return lax.dot_general(
        a, b, dims(ta, tb), precision=lax.Precision.HIGHEST, preferred_element_type=F32
    )


def half_dot(a, b):
    return lax.dot_general(a, b, dims(False, False), preferred_element_type=F32)


def split(x):
    high = x.astype(BF16)
    return high, (x - high.astype(F32)).astype(BF16)


def triangle_inverse(gramian):
    n = gramian.shape[0]
    r = lax.broadcasted_iota(jnp.int32, (n, n), 0)
    c = lax.broadcasted_iota(jnp.int32, (n, n), 1)
    eye = jnp.where(r == c, 1.0, 0.0).astype(F32)
    diagonal = jnp.where(r == c, gramian, 0.0)
    by_row = 2.0 / jnp.sum(diagonal, axis=1, keepdims=True)
    by_column = 2.0 / jnp.sum(diagonal, axis=0, keepdims=True)
    scaled = jnp.where(r > c, gramian * by_row, 0.0)
    power = jnp.where(r // 32 == c // 32, -scaled, 0.0)
    inverse = eye + power
    reach = 2
    while reach < 32:
        power = full_dot(power, power)
        inverse = inverse + full_dot(inverse, power)
        reach *= 2
    size = 32
    while size < n:
        rb, cb = r // size, c // size
        corner = jnp.where((rb == cb + 1) & (rb % 2 == 1), scaled, 0.0)
        inverse = inverse - full_dot(inverse, full_dot(corner, inverse))
        size *= 2
    return inverse * by_column, eye


def leaf_kernel(w_ref, a_ref):
    w = w_ref[0]
    inverse, eye = triangle_inverse(full_dot(w, w, False, True))
    a_ref[0] = eye - full_dot(full_dot(w, inverse, True, False), w)


def tree_kernel(w_ref, far_ref, p_ref):
    w, far = w_ref[0], far_ref[0]
    inverse, eye = triangle_inverse(
        full_dot(w, w, False, True) + full_dot(far, far, False, True)
    )
    m = full_dot(w, inverse, True, False)
    p_ref[0, :, :256] = eye - full_dot(m, w)
    p_ref[0, :, 256:] = -full_dot(m, far)


def main_kernel(x_ref, p_ref, o_ref, held, came, high, low, send_sem, recv_sem):
    row, col = lax.axis_index("row"), lax.axis_index("col")
    width = x_ref.shape[1] // CHUNKS

    def partner(level):
        s = 2 ** (level % LEVELS)
        return (row + s * (1 - 2 * ((row // s) % 2)), col)

    barrier = pltpu.get_barrier_semaphore()
    for level in range(LEVELS):
        pl.semaphore_signal(
            barrier, inc=1, device_id=partner(level), device_id_type=pl.DeviceIdType.MESH
        )
    pl.semaphore_wait(barrier, LEVELS)

    def columns(q):
        return pl.ds(pl.multiple_of(q * width, width), width)

    def copy(level, q):
        source = x_ref if level == 0 else held.at[level - 1]
        return pltpu.make_async_remote_copy(
            src_ref=source.at[:, columns(q)],
            dst_ref=came.at[level, :, columns(q)],
            send_sem=send_sem.at[level, q],
            recv_sem=recv_sem.at[level, q],
            device_id=partner(level),
            device_id_type=pl.DeviceIdType.MESH,
        )

    def first(q, _):
        copy(0, q).start()
        return 0

    lax.fori_loop(0, CHUNKS, first, 0)
    for level in range(2 * LEVELS):
        high[...], low[...] = split(p_ref[level])

        def step(q, _, level=level):
            copy(level, q).wait_recv()
            source = x_ref if level == 0 else held.at[level - 1]
            both = jnp.concatenate(
                [source[:, columns(q)], came[level, :, columns(q)]], axis=0
            )
            both_high, both_low = split(both)
            out = half_dot(high[...], both_high) + (
                half_dot(high[...], both_low) + half_dot(low[...], both_high)
            )
            if level == 2 * LEVELS - 1:
                o_ref[:, columns(q)] = out
            else:
                held[level, :, columns(q)] = out
                copy(level + 1, q).start()
            return 0

        lax.fori_loop(0, CHUNKS, step, 0)
    for level in range(2 * LEVELS):

        def last(q, _, level=level):
            copy(level, q).wait_send()
            return 0

        lax.fori_loop(0, CHUNKS, last, 0)


def swapped(value, level):
    mask = 2**level
    pairs = [(source, source ^ mask) for source in range(lax.axis_size("row"))]
    return lax.ppermute(value, "row", pairs)


def per_device(window, leaf_y, tree_y):
    rows, width = window.shape
    n = tree_y.shape[2]
    leaves = jnp.swapaxes(leaf_y, 1, 2)
    trees = jnp.swapaxes(tree_y, 2, 3)
    far = jnp.stack([swapped(trees[:, level], level) for level in range(LEVELS)], 1)
    far_leaf = swapped(leaves[0], 0)
    own = jnp.concatenate(
        [leaves, far_leaf[None], trees.reshape(-1, *trees.shape[2:]), far.reshape(-1, *far.shape[2:])], 0
    )
    full = lax.all_gather(own, "col", axis=1, tiled=True)

    def block(index):
        return pl.BlockSpec((1, n, n), lambda i: (index + i, 0, 0))

    big = pltpu.CompilerParams(vmem_limit_bytes=32 * 2**20)
    reflect = pl.pallas_call(
        leaf_kernel,
        grid=(3,),
        in_specs=[block(0)],
        out_specs=block(0),
        out_shape=jax.ShapeDtypeStruct((3, n, n), F32),
        compiler_params=big,
        name="leaf_prep",
    )(full)
    pairs = pl.pallas_call(
        tree_kernel,
        grid=(2 * LEVELS,),
        in_specs=[block(3), block(3 + 2 * LEVELS)],
        out_specs=pl.BlockSpec((1, n, 2 * n), lambda i: (i, 0, 0)),
        out_shape=jax.ShapeDtypeStruct((2 * LEVELS, n, 2 * n), F32),
        compiler_params=big,
        name="tree_prep",
    )(full, full)
    first = jnp.concatenate(
        [full_dot(pairs[0, :, :n], reflect[0]), full_dot(pairs[0, :, n:], reflect[2])], 1
    )
    middle = full_dot(reflect[1], pairs[LEVELS - 1])
    pairs = pairs.at[0].set(first).at[LEVELS - 1].set(middle)
    return pl.pallas_call(
        main_kernel,
        out_shape=jax.ShapeDtypeStruct(window.shape, F32),
        in_specs=[pl.BlockSpec(memory_space=pltpu.VMEM)] * 2,
        out_specs=pl.BlockSpec(memory_space=pltpu.VMEM),
        scratch_shapes=[
            pltpu.VMEM((2 * LEVELS - 1, rows, width), F32),
            pltpu.VMEM((2 * LEVELS, rows, width), F32),
            pltpu.VMEM((n, 2 * n), BF16),
            pltpu.VMEM((n, 2 * n), BF16),
            pltpu.SemaphoreType.DMA((2 * LEVELS, CHUNKS)),
            pltpu.SemaphoreType.DMA((2 * LEVELS, CHUNKS)),
        ],
        compiler_params=pltpu.CompilerParams(
            collective_id=0, has_side_effects=True, vmem_limit_bytes=48 * 2**20
        ),
        name="exchange",
    )(window, pairs)


def solution(mesh):
    return jax.shard_map(
        per_device,
        mesh=mesh,
        in_specs=(P("row", "col"), P(None, "row", "col"), P(None, None, "row", "col")),
        out_specs=P("row", "col"),
        check_vma=False,
    )
```

```python
import jax
import jax.numpy as jnp
from jax import lax
from jax.experimental import pallas as pl
from jax.experimental.pallas import tpu as pltpu
from jax.sharding import PartitionSpec as P

F32 = jnp.float32
BF16 = jnp.bfloat16
MESH = pl.DeviceIdType.MESH
LEVELS = 5
STEPS = 2 * LEVELS
CHUNKS = 8
GROUPS = 4
LAG = 1
PREP_AT = 3
LEAF = STEPS
SMALL = 32


def full_dot(a, b, ta=False, tb=False):
    dims = (((0,) if ta else (1,), (1,) if tb else (0,)), ((), ()))
    return lax.dot_general(
        a, b, dims, precision=lax.Precision.HIGHEST, preferred_element_type=F32
    )


def half_dot(a, b):
    return jnp.dot(a, b, preferred_element_type=F32)


def split(x):
    high = x.astype(BF16)
    return high, (x - high.astype(F32)).astype(BF16)


def iotas(m, n):
    return (
        lax.broadcasted_iota(jnp.int32, (m, n), 0),
        lax.broadcasted_iota(jnp.int32, (m, n), 1),
    )


def identity(n):
    r, c = iotas(n, n)
    return jnp.where(r == c, 1.0, 0.0)


def spread(blocks):
    s, n = blocks.shape
    r, c = iotas(n, n)
    return jnp.where(r // s == c // s, jnp.concatenate([blocks] * (n // s), axis=0), 0.0)


def fold(matrix, s):
    total = matrix[:s]
    for k in range(1, matrix.shape[0] // s):
        total = total + matrix[k * s : (k + 1) * s]
    return total


def triangle_inverse(gramian):
    n = gramian.shape[0]
    r, c = iotas(n, n)
    diagonal = jnp.where(r == c, gramian, 0.0)
    by_row = 2.0 / jnp.sum(diagonal, axis=1, keepdims=True)
    by_column = 2.0 / jnp.sum(diagonal, axis=0, keepdims=True)
    scaled = jnp.where(r > c, gramian * by_row, 0.0)
    s = SMALL
    power = fold(jnp.where(r // s == c // s, -scaled, 0.0), s)
    rs, cs = iotas(s, n)
    inverse = jnp.where(cs % s == rs, 1.0, 0.0) + power
    power = full_dot(power, spread(power))
    reach = 4
    while reach < s:
        both = full_dot(jnp.concatenate([power, inverse], 0), spread(power))
        power = both[:s]
        inverse = inverse + both[s:]
        reach *= 2
    inverse = inverse + full_dot(inverse, spread(power))
    while s < n // 2:
        corner = fold(
            jnp.where((r // s == c // s + 1) & ((r // s) % 2 == 1), scaled, 0.0), s
        )
        upper = full_dot(corner, spread(inverse))
        after = jnp.concatenate([inverse[:, s:], inverse[:, :s]], axis=1)
        lower = full_dot(after, spread(upper))
        even = (iotas(s, n)[1] // s) % 2 == 0
        inverse = jnp.concatenate(
            [jnp.where(even, inverse, 0.0), jnp.where(even, -lower, inverse)], axis=0
        )
        s *= 2
    first, second = inverse[:, :s], inverse[:, s:]
    lower = full_dot(second, full_dot(scaled[s:, :s], first))
    top = jnp.concatenate([first, jnp.zeros((s, s), F32)], 1)
    return jnp.concatenate([top, jnp.concatenate([-lower, second], 1)], 0) * by_column


def kernel(
    x_ref, own_ref, o_ref, held, came, high, low, wide, far, leaf,
    send_x, recv_x, send_hop, recv_hop, send_own, recv_own, send_far, recv_far,
):
    row, col = lax.axis_index("row"), lax.axis_index("col")
    n_col = lax.axis_size("col")
    part, n = own_ref.shape[1], own_ref.shape[2]
    width = x_ref.shape[1] // CHUNKS

    def partner(level):
        m = level % LEVELS
        s = (
            1 + m + m * (m - 1) // 2 + m * (m - 1) * (m - 2) // 6
            + m * (m - 1) * (m - 2) * (m - 3) // 24
        )
        return (row + s * (1 - 2 * ((row // s) % 2)), col)

    barrier = pltpu.get_barrier_semaphore()
    for level in range(LEVELS):
        pl.semaphore_signal(barrier, inc=1, device_id=partner(level), device_id_type=MESH)
    for d in range(1, n_col):
        pl.semaphore_signal(
            barrier, inc=1, device_id=(row, (col + d) % n_col), device_id_type=MESH
        )
    pl.semaphore_wait(barrier, LEVELS + n_col - 1)

    def columns(q):
        return pl.ds(pl.multiple_of(q * width, width), width)

    def exchange(source, level, q):
        return pltpu.make_async_remote_copy(
            src_ref=source.at[:, columns(q)],
            dst_ref=came.at[level, :, columns(q)],
            send_sem=send_x.at[level, q],
            recv_sem=recv_x.at[level, q],
            device_id=partner(level),
            device_id_type=MESH,
        )

    def hop(stage, level):
        return pltpu.make_async_remote_copy(
            src_ref=own_ref.at[stage],
            dst_ref=far.at[stage],
            send_sem=send_hop.at[stage],
            recv_sem=recv_hop.at[stage],
            device_id=partner(level),
            device_id_type=MESH,
        )

    mine = pl.ds(pl.multiple_of(col * part, part), part)

    def share(source, stage, lanes, send, recv):
        wide[stage, mine, lanes] = source[stage]

        def one(d, _):
            pltpu.make_async_remote_copy(
                src_ref=source.at[stage],
                dst_ref=wide.at[stage, mine, lanes],
                send_sem=send.at[stage],
                recv_sem=recv.at[stage],
                device_id=(row, (col + d) % n_col),
                device_id_type=MESH,
            ).start()
            return 0

        lax.fori_loop(1, n_col, one, 0)

    own_lanes, far_lanes = pl.ds(0, n), pl.ds(n, n)

    def all_shared(stage, lanes, send, recv):
        rows = pl.ds(0, (n_col - 1) * part)
        return pltpu.make_async_remote_copy(
            src_ref=wide.at[stage, rows, lanes],
            dst_ref=wide.at[stage, rows, lanes],
            send_sem=send.at[stage],
            recv_sem=recv.at[stage],
            device_id=(row, (col + 1) % n_col),
            device_id_type=MESH,
        )

    def share_own(stage):
        share(own_ref, stage, own_lanes, send_own, recv_own)

    def share_far(stage):
        hop(stage, 0).wait_recv()
        share(far, stage, far_lanes, send_far, recv_far)

    def leaf_reflection(i):
        lanes = pl.ds(pl.multiple_of((i % 2) * n, n), n)
        w = wide[LEAF + i // 2, :, lanes]
        inverse = triangle_inverse(full_dot(w, w, False, True))
        leaf[i] = identity(n) - full_dot(full_dot(w, inverse, True, False), w)

    hop(LEAF, 0).start()
    hop(0, 0).start()
    share_own(LEAF)

    def start_hop(stage, _):
        hop(stage, stage).start()
        return 0

    lax.fori_loop(1, STEPS, start_hop, 0)

    def start_window(q, _):
        exchange(x_ref, 0, q).start()
        return 0

    lax.fori_loop(0, CHUNKS, start_window, 0)
    share_far(LEAF)
    share_own(0)
    share_far(0)
    held[0] = x_ref[...]

    all_shared(LEAF, own_lanes, send_own, recv_own).wait_recv()

    def start_leaf(i, _):
        leaf_reflection(i)

        @pl.when(i == 0)
        def _():
            def rest(stage, _):
                share_own(stage)
                share_far(stage)
                return 0

            lax.fori_loop(1, LEVELS, rest, 0)
            share_own(LEAF + 1)
            lax.fori_loop(LEVELS, STEPS, rest, 0)
            all_shared(LEAF, far_lanes, send_far, recv_far).wait_recv()

        return 0

    lax.fori_loop(0, 2, start_leaf, 0)

    def prepare(level):
        all_shared(level, own_lanes, send_own, recv_own).wait_recv()
        all_shared(level, far_lanes, send_far, recv_far).wait_recv()
        both = wide[level]
        inverse = triangle_inverse(full_dot(both, both, False, True))
        out = full_dot(full_dot(both[:, :n], inverse, True, False), both)
        near, other = identity(n) - out[:, :n], -out[:, n:]

        def keep(lanes, matrix):
            high[level, :, lanes], low[level, :, lanes] = split(matrix)

        keep(own_lanes, near)
        keep(far_lanes, other)

        @pl.when(level == 0)
        def _():
            keep(own_lanes, full_dot(near, leaf[0]))
            keep(far_lanes, full_dot(other, leaf[1]))

        @pl.when(level == LEVELS - 1)
        def _():
            all_shared(LEAF + 1, own_lanes, send_own, recv_own).wait_recv()
            leaf_reflection(2)
            keep(own_lanes, full_dot(leaf[2], near))
            keep(far_lanes, full_dot(leaf[2], other))

    def advance(level, q):
        exchange(x_ref, level, q).wait_recv()
        both = jnp.concatenate(
            [held[level, :, columns(q)], came[level, :, columns(q)]], axis=0
        )
        both_high, both_low = split(both)
        out = half_dot(high[level], both_high) + (
            half_dot(high[level], both_low) + half_dot(low[level], both_high)
        )

        @pl.when(level == STEPS - 1)
        def _():
            o_ref[:, columns(q)] = out

        @pl.when(level < STEPS - 1)
        def _():
            held[level + 1, :, columns(q)] = out
            exchange(held.at[level + 1], level + 1, q).start()

    def wave(u, _):
        def item(q, _):
            level = u - 1 - LAG * (q // (CHUNKS // GROUPS))

            @pl.when((level >= 0) & (level < STEPS))
            def _():
                advance(level, q)

            return 0

        lax.fori_loop(0, PREP_AT, item, 0)

        @pl.when(u < STEPS)
        def _():
            prepare(u)

        lax.fori_loop(PREP_AT, CHUNKS, item, 0)
        return 0

    lax.fori_loop(0, STEPS + LAG * (GROUPS - 1) + 1, wave, 0)

    def drain_x(level, _):
        def one(q, _):
            exchange(x_ref, level, q).wait_send()
            return 0

        return lax.fori_loop(0, CHUNKS, one, 0)

    lax.fori_loop(0, STEPS, drain_x, 0)

    def drain_shares(stage, _):
        hop(stage, 0).wait_send()
        all_shared(stage, own_lanes, send_own, recv_own).wait_send()
        all_shared(stage, far_lanes, send_far, recv_far).wait_send()
        return 0

    lax.fori_loop(0, STEPS + 1, drain_shares, 0)
    all_shared(LEAF + 1, own_lanes, send_own, recv_own).wait_send()


def per_device(window, leaf_y, tree_y):
    rows, width = window.shape
    n, part = tree_y.shape[2:]
    own = jnp.concatenate([tree_y.reshape(STEPS, n, part), leaf_y], 0)
    own = jnp.swapaxes(own, 1, 2)
    dma = pltpu.SemaphoreType.DMA
    return pl.pallas_call(
        kernel,
        out_shape=jax.ShapeDtypeStruct(window.shape, F32),
        in_specs=[pl.BlockSpec(memory_space=pltpu.VMEM)] * 2,
        out_specs=pl.BlockSpec(memory_space=pltpu.VMEM),
        scratch_shapes=[
            pltpu.VMEM((STEPS, rows, width), F32),
            pltpu.VMEM((STEPS, rows, width), F32),
            pltpu.VMEM((STEPS, n, 2 * n), BF16),
            pltpu.VMEM((STEPS, n, 2 * n), BF16),
            pltpu.VMEM((STEPS + 2, n, 2 * n), F32),
            pltpu.VMEM((STEPS + 1, part, n), F32),
            pltpu.VMEM((3, n, n), F32),
            dma((STEPS, CHUNKS)),
            dma((STEPS, CHUNKS)),
            dma((STEPS + 1,)),
            dma((STEPS + 1,)),
            dma((STEPS + 2,)),
            dma((STEPS + 2,)),
            dma((STEPS + 1,)),
            dma((STEPS + 1,)),
        ],
        compiler_params=pltpu.CompilerParams(
            collective_id=0, has_side_effects=True, vmem_limit_bytes=56 * 2**20
        ),
        name="panels",
    )(window, own)


def solution(mesh):
    return jax.shard_map(
        per_device,
        mesh=mesh,
        in_specs=(P("row", "col"), P(None, "row", "col"), P(None, None, "row", "col")),
        out_specs=P("row", "col"),
        check_vma=False,
    )
```

```python
import jax
import jax.numpy as jnp
from jax import lax
from jax.experimental import pallas as pl
from jax.experimental.pallas import tpu as pltpu
from jax.sharding import PartitionSpec as P

F32 = jnp.float32
BF16 = jnp.bfloat16
MESH = pl.DeviceIdType.MESH
LEVELS = 5
STEPS = 2 * LEVELS
CHUNKS = 8
GROUPS = 4
LAG = 1
PREP_AT = 3
LEAF = STEPS
SMALL = 32
TURN = 2
TURNS = (TURN, TURN + LEVELS)
SWAPS = (TURN, TURN + LEVELS + 1)
EXTRA = {3: (11, 12), 4: (13, 14), 11: (15, None), 5: (16, 17), 6: (18, 19)}
SLOTS = 20


def at_least(value, bound):
    return (value + 32 - bound) // 32


def equal(value, bound):
    return at_least(value, bound) - at_least(value, bound + 1)


def core_level(level):
    return equal(level, TURNS[0]) + equal(level, TURNS[1])


def full_dot(a, b, ta=False, tb=False):
    dims = (((0,) if ta else (1,), (1,) if tb else (0,)), ((), ()))
    return lax.dot_general(
        a, b, dims, precision=lax.Precision.HIGHEST, preferred_element_type=F32
    )


def half_dot(a, b):
    return jnp.dot(a, b, preferred_element_type=F32)


def split(x):
    high = x.astype(BF16)
    return high, (x - high.astype(F32)).astype(BF16)


def iotas(m, n):
    return (
        lax.broadcasted_iota(jnp.int32, (m, n), 0),
        lax.broadcasted_iota(jnp.int32, (m, n), 1),
    )


def identity(n):
    r, c = iotas(n, n)
    return jnp.where(r == c, 1.0, 0.0)


def spread(blocks):
    s, n = blocks.shape
    r, c = iotas(n, n)
    return jnp.where(r // s == c // s, jnp.concatenate([blocks] * (n // s), axis=0), 0.0)


def fold(matrix, s):
    total = matrix[:s]
    for k in range(1, matrix.shape[0] // s):
        total = total + matrix[k * s : (k + 1) * s]
    return total


def triangle_inverse(gramian):
    n = gramian.shape[0]
    r, c = iotas(n, n)
    diagonal = jnp.where(r == c, gramian, 0.0)
    by_row = 2.0 / jnp.sum(diagonal, axis=1, keepdims=True)
    by_column = 2.0 / jnp.sum(diagonal, axis=0, keepdims=True)
    scaled = jnp.where(r > c, gramian * by_row, 0.0)
    s = SMALL
    power = fold(jnp.where(r // s == c // s, -scaled, 0.0), s)
    rs, cs = iotas(s, n)
    inverse = jnp.where(cs % s == rs, 1.0, 0.0) + power
    power = full_dot(power, spread(power))
    reach = 4
    while reach < s:
        both = full_dot(jnp.concatenate([power, inverse], 0), spread(power))
        power = both[:s]
        inverse = inverse + both[s:]
        reach *= 2
    inverse = inverse + full_dot(inverse, spread(power))
    while s < n // 2:
        corner = fold(
            jnp.where((r // s == c // s + 1) & ((r // s) % 2 == 1), scaled, 0.0), s
        )
        upper = full_dot(corner, spread(inverse))
        after = jnp.concatenate([inverse[:, s:], inverse[:, :s]], axis=1)
        lower = full_dot(after, spread(upper))
        even = (iotas(s, n)[1] // s) % 2 == 0
        inverse = jnp.concatenate(
            [jnp.where(even, inverse, 0.0), jnp.where(even, -lower, inverse)], axis=0
        )
        s *= 2
    first, second = inverse[:, :s], inverse[:, s:]
    lower = full_dot(second, full_dot(scaled[s:, :s], first))
    top = jnp.concatenate([first, jnp.zeros((s, s), F32)], 1)
    return jnp.concatenate([top, jnp.concatenate([-lower, second], 1)], 0) * by_column


def kernel(
    x_ref, own_ref, o_ref, held, came, high, low, wide, far, leaf,
    send_x, recv_x, send_swap, recv_swap, send_hop, recv_hop,
    send_near, recv_near, send_far, recv_far,
):
    row, col = lax.axis_index("row"), lax.axis_index("col")
    n_col = lax.axis_size("col")
    part, n = own_ref.shape[1], own_ref.shape[2]
    width = x_ref.shape[1] // CHUNKS

    def towards(m):
        s = (
            1 + m + m * (m - 1) // 2 + m * (m - 1) * (m - 2) // 6
            + m * (m - 1) * (m - 2) * (m - 3) // 24
        )
        return s * (1 - 2 * ((row // s) % 2))

    def moved_of(any_col):
        return ((row // 2**TURN) % 2 + any_col) % 2

    moved = moved_of(col)
    sibling = col + 1 - 2 * (col % 2)
    across = row + towards(TURN)

    def partner(level):
        return (
            row + (1 - core_level(level)) * towards(level % LEVELS),
            col + core_level(level) * (sibling - col),
        )

    greeted = [(row + towards(m), col) for m in range(LEVELS)]
    greeted += [(across + towards(m), col) for m in range(LEVELS) if m != TURN]
    greeted += [(across, sibling)] + [(row, (col + d) % n_col) for d in range(1, n_col)]
    barrier = pltpu.get_barrier_semaphore()
    for other in greeted:
        pl.semaphore_signal(barrier, inc=1, device_id=other, device_id_type=MESH)
    pl.semaphore_wait(barrier, len(greeted))

    def columns(q):
        return pl.ds(pl.multiple_of(q * width, width), width)

    def exchange(source, level, q):
        return pltpu.make_async_remote_copy(
            src_ref=source.at[:, columns(q)],
            dst_ref=came.at[level, :, columns(q)],
            send_sem=send_x.at[level, q],
            recv_sem=recv_x.at[level, q],
            device_id=partner(level),
            device_id_type=MESH,
        )

    def swap(way, q):
        return pltpu.make_async_remote_copy(
            src_ref=held.at[SWAPS[0] + way * (SWAPS[1] - SWAPS[0]), :, columns(q)],
            dst_ref=held.at[STEPS + way, :, columns(q)],
            send_sem=send_swap.at[way, q],
            recv_sem=recv_swap.at[way, q],
            device_id=(across, sibling),
            device_id_type=MESH,
        )

    def hop(stage, slot, to_row):
        return pltpu.make_async_remote_copy(
            src_ref=own_ref.at[stage],
            dst_ref=far.at[slot],
            send_sem=send_hop.at[slot],
            recv_sem=recv_hop.at[slot],
            device_id=(to_row, col),
            device_id_type=MESH,
        )

    mine = pl.ds(pl.multiple_of(col * part, part), part)
    near_lanes, far_lanes = pl.ds(0, n), pl.ds(n, n)

    def share(stage, lanes, kept, other, send, recv):
        def to(source, d):
            pltpu.make_async_remote_copy(
                src_ref=source,
                dst_ref=wide.at[stage, mine, lanes],
                send_sem=send.at[stage],
                recv_sem=recv.at[stage],
                device_id=(row, (col + d) % n_col),
                device_id_type=MESH,
            ).start()

        def one(d, _):
            if other is None:
                to(kept, d)
            else:
                away = moved_of(col + d)

                @pl.when(away == 0)
                def _():
                    to(kept, d)

                @pl.when(away == 1)
                def _():
                    to(other, d)

            return 0

        lax.fori_loop(1, n_col, one, 0)
        if other is None:
            wide[stage, mine, lanes] = kept[...]
        else:

            @pl.when(moved == 0)
            def _():
                wide[stage, mine, lanes] = kept[...]

            @pl.when(moved == 1)
            def _():
                wide[stage, mine, lanes] = other[...]

    def arrive(slot):
        hop(0, slot, row + towards(0)).wait_recv()

    def share_both(stage):
        own = own_ref.at[stage]
        if stage == LEAF + 1:
            arrive(EXTRA[stage][0])
            share(stage, near_lanes, own, far.at[EXTRA[stage][0]], send_near, recv_near)
            return
        if stage in EXTRA:
            near_slot, far_slot = EXTRA[stage]
            arrive(near_slot)
            share(stage, near_lanes, own, far.at[near_slot], send_near, recv_near)
            arrive(stage)
            arrive(far_slot)
            share(stage, far_lanes, far.at[stage], far.at[far_slot], send_far, recv_far)
            return
        if stage in TURNS:
            arrive(stage)
            share(stage, near_lanes, own, far.at[stage], send_near, recv_near)
            share(stage, far_lanes, far.at[stage], own, send_far, recv_far)
            return
        share(stage, near_lanes, own, None, send_near, recv_near)
        arrive(stage)
        share(stage, far_lanes, far.at[stage], None, send_far, recv_far)

    def all_shared(stage, lanes, send, recv):
        rows = pl.ds(0, (n_col - 1) * part)
        return pltpu.make_async_remote_copy(
            src_ref=wide.at[stage, rows, lanes],
            dst_ref=wide.at[stage, rows, lanes],
            send_sem=send.at[stage],
            recv_sem=recv.at[stage],
            device_id=(row, sibling),
            device_id_type=MESH,
        )

    def leaf_reflection(i):
        lanes = pl.ds(pl.multiple_of((i % 2) * n, n), n)
        w = wide[LEAF + i // 2, :, lanes]
        inverse = triangle_inverse(full_dot(w, w, False, True))
        leaf[i] = identity(n) - full_dot(full_dot(w, inverse, True, False), w)

    hop(LEAF, LEAF, row + towards(0)).start()
    hop(0, 0, row + towards(0)).start()
    share(LEAF, near_lanes, own_ref.at[LEAF], None, send_near, recv_near)
    for stage in (1, 2, 7, 8, 9):
        hop(stage, stage, row + towards(stage % LEVELS)).start()

    def start_window(q, _):
        exchange(x_ref, 0, q).start()
        return 0

    lax.fori_loop(0, CHUNKS, start_window, 0)
    arrive(LEAF)
    share(LEAF, far_lanes, far.at[LEAF], None, send_far, recv_far)
    share_both(0)
    for stage, slots in EXTRA.items():
        hop(stage, slots[0], across).start()
        if stage < STEPS:
            hop(stage, stage, row + towards(stage % LEVELS)).start()
            hop(stage, slots[1], across + towards(stage % LEVELS)).start()
    held[0] = x_ref[...]

    all_shared(LEAF, near_lanes, send_near, recv_near).wait_recv()

    def start_leaf(i, _):
        leaf_reflection(i)

        @pl.when(i == 0)
        def _():
            for stage in (1, 2, 7, 8, 9):
                share_both(stage)
            all_shared(LEAF, far_lanes, send_far, recv_far).wait_recv()

        return 0

    lax.fori_loop(0, 2, start_leaf, 0)

    def prepare(level):
        all_shared(level, near_lanes, send_near, recv_near).wait_recv()
        all_shared(level, far_lanes, send_far, recv_far).wait_recv()
        both = wide[level]
        inverse = triangle_inverse(full_dot(both, both, False, True))
        out = full_dot(full_dot(both[:, :n], inverse, True, False), both)
        near, other = identity(n) - out[:, :n], -out[:, n:]

        def keep(lanes, matrix):
            high[level, :, lanes], low[level, :, lanes] = split(matrix)

        keep(near_lanes, near)
        keep(far_lanes, other)

        @pl.when(level == 0)
        def _():
            keep(near_lanes, full_dot(near, leaf[0]))
            keep(far_lanes, full_dot(other, leaf[1]))

        @pl.when(level == LEVELS - 1)
        def _():
            all_shared(LEAF + 1, near_lanes, send_near, recv_near).wait_recv()
            leaf_reflection(2)
            keep(near_lanes, full_dot(leaf[2], near))
            keep(far_lanes, full_dot(leaf[2], other))

    def advance(level, q):
        exchange(x_ref, level, q).wait_recv()
        slot = level + moved * (
            equal(level, SWAPS[0]) * (STEPS - SWAPS[0])
            + equal(level, SWAPS[1]) * (STEPS + 1 - SWAPS[1])
        )
        both = jnp.concatenate(
            [held[slot, :, columns(q)], came[level, :, columns(q)]], axis=0
        )
        both_high, both_low = split(both)
        out = half_dot(high[level], both_high) + (
            half_dot(high[level], both_low) + half_dot(low[level], both_high)
        )
        swaps = moved * (equal(level, SWAPS[0] - 1) + equal(level, SWAPS[1] - 1))

        @pl.when(level == STEPS - 1)
        def _():
            o_ref[:, columns(q)] = out

        @pl.when(level < STEPS - 1)
        def _():
            held[level + 1, :, columns(q)] = out

            @pl.when(swaps == 0)
            def _():
                exchange(held.at[level + 1], level + 1, q).start()

            @pl.when(swaps == 1)
            def _():
                swap(equal(level, SWAPS[1] - 1), q).start()

    def settle(way, q):
        @pl.when(moved == 1)
        def _():
            swap(way, q).wait_recv()
            exchange(held.at[STEPS + way], SWAPS[0] + way * (SWAPS[1] - SWAPS[0]), q).start()

    def item(step, q):
        way = at_least(step, SWAPS[1] + 1)
        level = step - at_least(step, SWAPS[0] + 1) - at_least(step, SWAPS[1] + 2)
        swapping = equal(step, SWAPS[0]) + equal(step, SWAPS[1] + 1)

        @pl.when(swapping == 1)
        def _():
            settle(way, q)

        @pl.when(swapping == 0)
        def _():
            advance(level, q)

    def wave(u, _):
        def one(q, _):
            step = u - 1 - LAG * (q // (CHUNKS // GROUPS))

            @pl.when((step >= 0) & (step < STEPS + 2))
            def _():
                item(step, q)

            return 0

        lax.fori_loop(0, PREP_AT, one, 0)
        swapping = equal(u, SWAPS[0]) + equal(u, SWAPS[1] + 1)

        @pl.when((u < STEPS + 2) & (swapping == 0))
        def _():
            prepare(u - at_least(u, SWAPS[0] + 1) - at_least(u, SWAPS[1] + 2))

        @pl.when(u == SWAPS[0])
        def _():
            for stage in EXTRA:
                share_both(stage)

        lax.fori_loop(PREP_AT, CHUNKS, one, 0)
        return 0

    lax.fori_loop(0, STEPS + 2 + LAG * (GROUPS - 1) + 1, wave, 0)

    def drain_x(level, _):
        def one(q, _):
            exchange(x_ref, level, q).wait_send()
            return 0

        return lax.fori_loop(0, CHUNKS, one, 0)

    lax.fori_loop(0, STEPS, drain_x, 0)

    @pl.when(moved == 1)
    def _():
        def drain_swap(q, _):
            swap(0, q).wait_send()
            swap(1, q).wait_send()
            return 0

        lax.fori_loop(0, CHUNKS, drain_swap, 0)

    def drain_hop(slot, _):
        hop(0, slot, row + towards(0)).wait_send()
        return 0

    lax.fori_loop(0, SLOTS, drain_hop, 0)

    def drain_shares(stage, _):
        all_shared(stage, near_lanes, send_near, recv_near).wait_send()
        all_shared(stage, far_lanes, send_far, recv_far).wait_send()
        return 0

    lax.fori_loop(0, STEPS + 1, drain_shares, 0)
    all_shared(LEAF + 1, near_lanes, send_near, recv_near).wait_send()


def per_device(window, leaf_y, tree_y):
    rows, width = window.shape
    n, part = tree_y.shape[2:]
    own = jnp.concatenate([tree_y.reshape(STEPS, n, part), leaf_y], 0)
    own = jnp.swapaxes(own, 1, 2)
    dma = pltpu.SemaphoreType.DMA
    return pl.pallas_call(
        kernel,
        out_shape=jax.ShapeDtypeStruct(window.shape, F32),
        in_specs=[pl.BlockSpec(memory_space=pltpu.VMEM)] * 2,
        out_specs=pl.BlockSpec(memory_space=pltpu.VMEM),
        scratch_shapes=[
            pltpu.VMEM((STEPS + 2, rows, width), F32),
            pltpu.VMEM((STEPS, rows, width), F32),
            pltpu.VMEM((STEPS, n, 2 * n), BF16),
            pltpu.VMEM((STEPS, n, 2 * n), BF16),
            pltpu.VMEM((STEPS + 2, n, 2 * n), F32),
            pltpu.VMEM((SLOTS, part, n), F32),
            pltpu.VMEM((3, n, n), F32),
            dma((STEPS, CHUNKS)),
            dma((STEPS, CHUNKS)),
            dma((2, CHUNKS)),
            dma((2, CHUNKS)),
            dma((SLOTS,)),
            dma((SLOTS,)),
            dma((STEPS + 2,)),
            dma((STEPS + 2,)),
            dma((STEPS + 2,)),
            dma((STEPS + 2,)),
        ],
        compiler_params=pltpu.CompilerParams(
            collective_id=0, has_side_effects=True, vmem_limit_bytes=56 * 2**20
        ),
        name="panels",
    )(window, own)


def solution(mesh):
    return jax.shard_map(
        per_device,
        mesh=mesh,
        in_specs=(P("row", "col"), P(None, "row", "col"), P(None, None, "row", "col")),
        out_specs=P("row", "col"),
        check_vma=False,
    )
```

```python
import jax
import jax.numpy as jnp
from jax import lax
from jax.experimental import pallas as pl
from jax.experimental.pallas import tpu as pltpu
from jax.sharding import PartitionSpec as P

F32 = jnp.float32
BF16 = jnp.bfloat16
MESH = pl.DeviceIdType.MESH
LEVELS = 5
STEPS = 2 * LEVELS
CHUNKS = 8
ORDER = (
    16648, 21397905, 25740427, 58835603, 12878356, 44649885,
    63132204, 80447502, 111793807, 98945817, 65902647, 84283710,
    68279353, 138960945, 158356681, 89122091, 110008648, 125085904,
    160487892, 191962835, 127364429, 181824220, 165126854, 184135631,
    202781283, 221918177, 268432741,
)
LEAF = STEPS
SMALL = 32
TURN = 2
TURNS = (TURN, TURN + LEVELS)
SWAPS = (TURN, TURN + LEVELS + 1)
EXTRA = {3: (11, 12), 4: (13, 14), 11: (15, None), 5: (16, 17), 6: (18, 19)}
SLOTS = 20


def at_least(value, bound):
    return (value + 32 - bound) // 32


def equal(value, bound):
    return at_least(value, bound) - at_least(value, bound + 1)


def core_level(level):
    return equal(level, TURNS[0]) + equal(level, TURNS[1])


def full_dot(a, b, ta=False, tb=False):
    dims = (((0,) if ta else (1,), (1,) if tb else (0,)), ((), ()))
    return lax.dot_general(
        a, b, dims, precision=lax.Precision.HIGHEST, preferred_element_type=F32
    )


def half_dot(a, b):
    return jnp.dot(a, b, preferred_element_type=F32)


def split(x):
    high = x.astype(BF16)
    return high, (x - high.astype(F32)).astype(BF16)


def iotas(m, n):
    return (
        lax.broadcasted_iota(jnp.int32, (m, n), 0),
        lax.broadcasted_iota(jnp.int32, (m, n), 1),
    )


def identity(n):
    r, c = iotas(n, n)
    return jnp.where(r == c, 1.0, 0.0)


def spread(blocks):
    s, n = blocks.shape
    r, c = iotas(n, n)
    return jnp.where(r // s == c // s, jnp.concatenate([blocks] * (n // s), axis=0), 0.0)


def fold(matrix, s):
    total = matrix[:s]
    for k in range(1, matrix.shape[0] // s):
        total = total + matrix[k * s : (k + 1) * s]
    return total


def triangle_inverse(gramian):
    n = gramian.shape[0]
    r, c = iotas(n, n)
    diagonal = jnp.where(r == c, gramian, 0.0)
    by_row = 2.0 / jnp.sum(diagonal, axis=1, keepdims=True)
    by_column = 2.0 / jnp.sum(diagonal, axis=0, keepdims=True)
    scaled = jnp.where(r > c, gramian * by_row, 0.0)
    s = SMALL
    power = fold(jnp.where(r // s == c // s, -scaled, 0.0), s)
    rs, cs = iotas(s, n)
    inverse = jnp.where(cs % s == rs, 1.0, 0.0) + power
    power = full_dot(power, spread(power))
    reach = 4
    while reach < s:
        both = full_dot(jnp.concatenate([power, inverse], 0), spread(power))
        power = both[:s]
        inverse = inverse + both[s:]
        reach *= 2
    inverse = inverse + full_dot(inverse, spread(power))
    while s < n // 2:
        corner = fold(
            jnp.where((r // s == c // s + 1) & ((r // s) % 2 == 1), scaled, 0.0), s
        )
        upper = full_dot(corner, spread(inverse))
        after = jnp.concatenate([inverse[:, s:], inverse[:, :s]], axis=1)
        lower = full_dot(after, spread(upper))
        even = (iotas(s, n)[1] // s) % 2 == 0
        inverse = jnp.concatenate(
            [jnp.where(even, inverse, 0.0), jnp.where(even, -lower, inverse)], axis=0
        )
        s *= 2
    first, second = inverse[:, :s], inverse[:, s:]
    lower = full_dot(second, full_dot(scaled[s:, :s], first))
    top = jnp.concatenate([first, jnp.zeros((s, s), F32)], 1)
    return jnp.concatenate([top, jnp.concatenate([-lower, second], 1)], 0) * by_column


def kernel(
    x_ref, tree_ref, leaf_ref, o_ref, held, came, high, low, wide, far, leaf,
    send_x, recv_x, send_swap, recv_swap, send_hop, recv_hop,
    send_near, recv_near, send_far, recv_far, send_leaf, recv_leaf,
):
    row, col = lax.axis_index("row"), lax.axis_index("col")
    n_col = lax.axis_size("col")
    part, n = leaf_ref.shape[1:]
    width = x_ref.shape[1] // CHUNKS

    def towards(m):
        s = (
            1 + m + m * (m - 1) // 2 + m * (m - 1) * (m - 2) // 6
            + m * (m - 1) * (m - 2) * (m - 3) // 24
        )
        return s * (1 - 2 * ((row // s) % 2))

    def moved_of(any_col):
        return ((row // 2**TURN) % 2 + any_col) % 2

    moved = moved_of(col)
    sibling = col + 1 - 2 * (col % 2)
    across = row + towards(TURN)

    def partner(level):
        return (
            row + (1 - core_level(level)) * towards(level % LEVELS),
            col + core_level(level) * (sibling - col),
        )

    greeted = [(row + towards(m), col) for m in range(LEVELS)]
    greeted += [(across + towards(m), col) for m in range(LEVELS) if m != TURN]
    greeted += [(across, sibling)] + [(row, (col + d) % n_col) for d in range(1, n_col)]
    barrier = pltpu.get_barrier_semaphore()
    for other in greeted:
        pl.semaphore_signal(barrier, inc=1, device_id=other, device_id_type=MESH)
    pl.semaphore_wait(barrier, len(greeted))

    def columns(q):
        return pl.ds(pl.multiple_of(q * width, width), width)

    def exchange(source, level, q):
        return pltpu.make_async_remote_copy(
            src_ref=source.at[:, columns(q)],
            dst_ref=came.at[level, :, columns(q)],
            send_sem=send_x.at[level, q],
            recv_sem=recv_x.at[level, q],
            device_id=partner(level),
            device_id_type=MESH,
        )

    def swap(way, q):
        return pltpu.make_async_remote_copy(
            src_ref=held.at[SWAPS[0] + way * (SWAPS[1] - SWAPS[0]), :, columns(q)],
            dst_ref=held.at[STEPS + way, :, columns(q)],
            send_sem=send_swap.at[way, q],
            recv_sem=recv_swap.at[way, q],
            device_id=(across, sibling),
            device_id_type=MESH,
        )

    def own(stage):
        if stage < LEAF:
            return tree_ref.at[stage // LEVELS, stage % LEVELS]
        return leaf_ref.at[stage - LEAF]

    def hop(stage, slot, to_row):
        return pltpu.make_async_remote_copy(
            src_ref=own(stage),
            dst_ref=far.at[slot],
            send_sem=send_hop.at[slot],
            recv_sem=recv_hop.at[slot],
            device_id=(to_row, col),
            device_id_type=MESH,
        )

    mine = pl.ds(pl.multiple_of(col * part, part), part)
    near_lanes, far_lanes = pl.ds(0, n), pl.ds(n, n)

    def share(stage, lanes, kept, other, send, recv):
        def to(source, d):
            pltpu.make_async_remote_copy(
                src_ref=source,
                dst_ref=wide.at[stage, mine, lanes],
                send_sem=send.at[stage],
                recv_sem=recv.at[stage],
                device_id=(row, (col + d) % n_col),
                device_id_type=MESH,
            ).start()

        def one(d, _):
            if other is None:
                to(kept, d)
            else:
                away = moved_of(col + d)

                @pl.when(away == 0)
                def _():
                    to(kept, d)

                @pl.when(away == 1)
                def _():
                    to(other, d)

            return 0

        lax.fori_loop(1, n_col, one, 0)
        if other is None:
            wide[stage, mine, lanes] = kept[...]
        else:

            @pl.when(moved == 0)
            def _():
                wide[stage, mine, lanes] = kept[...]

            @pl.when(moved == 1)
            def _():
                wide[stage, mine, lanes] = other[...]

    def arrive(slot):
        hop(0, slot, row + towards(0)).wait_recv()

    def share_both(stage):
        if stage == LEAF + 1:
            arrive(EXTRA[stage][0])
            share(stage, near_lanes, own(stage), far.at[EXTRA[stage][0]], send_near, recv_near)
            return
        if stage in EXTRA:
            near_slot, far_slot = EXTRA[stage]
            arrive(near_slot)
            share(stage, near_lanes, own(stage), far.at[near_slot], send_near, recv_near)
            arrive(stage)
            arrive(far_slot)
            share(stage, far_lanes, far.at[stage], far.at[far_slot], send_far, recv_far)
            return
        if stage in TURNS:
            arrive(stage)
            share(stage, near_lanes, own(stage), far.at[stage], send_near, recv_near)
            share(stage, far_lanes, far.at[stage], own(stage), send_far, recv_far)
            return
        share(stage, near_lanes, own(stage), None, send_near, recv_near)
        arrive(stage)
        share(stage, far_lanes, far.at[stage], None, send_far, recv_far)

    def all_shared(stage, lanes, send, recv):
        rows = pl.ds(0, (n_col - 1) * part)
        return pltpu.make_async_remote_copy(
            src_ref=wide.at[stage, rows, lanes],
            dst_ref=wide.at[stage, rows, lanes],
            send_sem=send.at[stage],
            recv_sem=recv.at[stage],
            device_id=(row, sibling),
            device_id_type=MESH,
        )

    def leaf_reflection(i):
        lanes = pl.ds(pl.multiple_of((i % 2) * n, n), n)
        w = wide[LEAF + i // 2, :, lanes]
        inverse = triangle_inverse(full_dot(w, w, False, True))
        leaf[i] = identity(n) - full_dot(full_dot(w, inverse, True, False), w)

    hop(LEAF, LEAF, row + towards(0)).start()
    hop(0, 0, row + towards(0)).start()
    share(LEAF, near_lanes, own(LEAF), None, send_near, recv_near)
    for stage in (1, 2, 7, 8, 9):
        hop(stage, stage, row + towards(stage % LEVELS)).start()

    def start_window(q, _):
        exchange(x_ref, 0, q).start()
        return 0

    lax.fori_loop(0, CHUNKS, start_window, 0)
    arrive(LEAF)
    share(LEAF, far_lanes, far.at[LEAF], None, send_far, recv_far)
    share_both(0)
    for stage, slots in EXTRA.items():
        hop(stage, slots[0], across).start()
        if stage < STEPS:
            hop(stage, stage, row + towards(stage % LEVELS)).start()
            hop(stage, slots[1], across + towards(stage % LEVELS)).start()
    held[0] = x_ref[...]

    share_both(1)

    core = col % 2

    @pl.when(core == 0)
    def _():
        all_shared(LEAF, near_lanes, send_near, recv_near).wait_recv()

    @pl.when(core == 1)
    def _():
        all_shared(LEAF, far_lanes, send_far, recv_far).wait_recv()

    leaf_reflection(core)
    to_sibling = pltpu.make_async_remote_copy(
        src_ref=leaf.at[core],
        dst_ref=leaf.at[core],
        send_sem=send_leaf,
        recv_sem=recv_leaf,
        device_id=(row, sibling),
        device_id_type=MESH,
    )
    to_sibling.start()

    @pl.when(core == 1)
    def _():
        all_shared(LEAF, near_lanes, send_near, recv_near).wait_recv()

    @pl.when(core == 0)
    def _():
        all_shared(LEAF, far_lanes, send_far, recv_far).wait_recv()

    def prepare(level):
        all_shared(level, near_lanes, send_near, recv_near).wait_recv()
        all_shared(level, far_lanes, send_far, recv_far).wait_recv()
        both = wide[level]
        inverse = triangle_inverse(full_dot(both, both, False, True))
        out = full_dot(full_dot(both[:, :n], inverse, True, False), both)
        near, other = identity(n) - out[:, :n], -out[:, n:]

        def keep(lanes, matrix):
            high[level, :, lanes], low[level, :, lanes] = split(matrix)

        keep(near_lanes, near)
        keep(far_lanes, other)

        @pl.when(level == 0)
        def _():
            to_sibling.wait()
            keep(near_lanes, full_dot(near, leaf[0]))
            keep(far_lanes, full_dot(other, leaf[1]))

        @pl.when(level == LEVELS - 1)
        def _():
            all_shared(LEAF + 1, near_lanes, send_near, recv_near).wait_recv()
            leaf_reflection(2)
            keep(near_lanes, full_dot(leaf[2], near))
            keep(far_lanes, full_dot(leaf[2], other))

    def advance(level, q):
        exchange(x_ref, level, q).wait_recv()
        slot = level + moved * (
            equal(level, SWAPS[0]) * (STEPS - SWAPS[0])
            + equal(level, SWAPS[1]) * (STEPS + 1 - SWAPS[1])
        )
        both = jnp.concatenate(
            [held[slot, :, columns(q)], came[level, :, columns(q)]], axis=0
        )
        both_high, both_low = split(both)
        out = half_dot(high[level], both_high) + (
            half_dot(high[level], both_low) + half_dot(low[level], both_high)
        )
        swaps = moved * (equal(level, SWAPS[0] - 1) + equal(level, SWAPS[1] - 1))

        @pl.when(level == STEPS - 1)
        def _():
            o_ref[:, columns(q)] = out

        @pl.when(level < STEPS - 1)
        def _():
            held[level + 1, :, columns(q)] = out

            @pl.when(swaps == 0)
            def _():
                exchange(held.at[level + 1], level + 1, q).start()

            @pl.when(swaps == 1)
            def _():
                swap(equal(level, SWAPS[1] - 1), q).start()

    def settle(way, q):
        @pl.when(moved == 1)
        def _():
            swap(way, q).wait_recv()
            exchange(held.at[STEPS + way], SWAPS[0] + way * (SWAPS[1] - SWAPS[0]), q).start()

    def item(step, q):
        way = at_least(step, SWAPS[1] + 1)
        level = step - at_least(step, SWAPS[0] + 1) - at_least(step, SWAPS[1] + 2)
        swapping = equal(step, SWAPS[0]) + equal(step, SWAPS[1] + 1)

        @pl.when(swapping == 1)
        def _():
            settle(way, q)

        @pl.when(swapping == 0)
        def _():
            advance(level, q)

    def turn(w, _):
        word = jnp.int32(0)
        for k, entries in enumerate(ORDER):
            word = jnp.where(w == k, jnp.int32(entries), word)

        def one(_, left):
            entry = lax.rem(left, 128)
            what, count = lax.rem(entry, 9), lax.div(entry, 9)

            @pl.when((what < 8) & (count < STEPS + 2))
            def _():
                item(count, what)

            @pl.when((what == 8) & (count < STEPS))
            def _():
                @pl.when(count == 1)
                def _():
                    for stage in (2, 7, 8, 9):
                        share_both(stage)

                @pl.when(count == TURN)
                def _():
                    for stage in EXTRA:
                        share_both(stage)

                prepare(count)

            return lax.div(left, 128)

        lax.fori_loop(0, 4, one, word)
        return 0

    lax.fori_loop(0, len(ORDER), turn, 0)

    def drain_x(level, _):
        def one(q, _):
            exchange(x_ref, level, q).wait_send()
            return 0

        return lax.fori_loop(0, CHUNKS, one, 0)

    lax.fori_loop(0, STEPS, drain_x, 0)

    @pl.when(moved == 1)
    def _():
        def drain_swap(q, _):
            swap(0, q).wait_send()
            swap(1, q).wait_send()
            return 0

        lax.fori_loop(0, CHUNKS, drain_swap, 0)

    def drain_hop(slot, _):
        hop(0, slot, row + towards(0)).wait_send()
        return 0

    lax.fori_loop(0, SLOTS, drain_hop, 0)

    def drain_shares(stage, _):
        all_shared(stage, near_lanes, send_near, recv_near).wait_send()
        all_shared(stage, far_lanes, send_far, recv_far).wait_send()
        return 0

    lax.fori_loop(0, STEPS + 1, drain_shares, 0)
    all_shared(LEAF + 1, near_lanes, send_near, recv_near).wait_send()


def per_device(window, leaf_y, tree_y):
    rows, width = window.shape
    n, part = tree_y.shape[2:]
    dma = pltpu.SemaphoreType.DMA
    return pl.pallas_call(
        kernel,
        out_shape=jax.ShapeDtypeStruct(window.shape, F32),
        in_specs=[pl.BlockSpec(memory_space=pltpu.VMEM)] * 3,
        out_specs=pl.BlockSpec(memory_space=pltpu.VMEM),
        scratch_shapes=[
            pltpu.VMEM((STEPS + 2, rows, width), F32),
            pltpu.VMEM((STEPS, rows, width), F32),
            pltpu.VMEM((STEPS, n, 2 * n), BF16),
            pltpu.VMEM((STEPS, n, 2 * n), BF16),
            pltpu.VMEM((STEPS + 2, n, 2 * n), F32),
            pltpu.VMEM((SLOTS, part, n), F32),
            pltpu.VMEM((3, n, n), F32),
            dma((STEPS, CHUNKS)),
            dma((STEPS, CHUNKS)),
            dma((2, CHUNKS)),
            dma((2, CHUNKS)),
            dma((SLOTS,)),
            dma((SLOTS,)),
            dma((STEPS + 2,)),
            dma((STEPS + 2,)),
            dma((STEPS + 2,)),
            dma((STEPS + 2,)),
            dma,
            dma,
        ],
        compiler_params=pltpu.CompilerParams(
            collective_id=0, has_side_effects=True, vmem_limit_bytes=56 * 2**20
        ),
        name="panels",
    )(window, jnp.swapaxes(tree_y, 2, 3), jnp.swapaxes(leaf_y, 1, 2))


def solution(mesh):
    return jax.shard_map(
        per_device,
        mesh=mesh,
        in_specs=(P("row", "col"), P(None, "row", "col"), P(None, None, "row", "col")),
        out_specs=P("row", "col"),
        check_vma=False,
    )
```
